32 devices in a mesh: group: 4 (over y, core), tile: 8 (over z, x).
Axes of the slice: x: 2, y: 2, z: 4, core: 2. Of those that a mesh axis runs over, the one named last changes fastest.
Arguments:
- checkpoint: float32 [16, 512, 768], P(None, ('group', 'tile')), may hold values from -6 to 6
- adjoint_in: float32 [16, 512, 768], P(None, ('group', 'tile')), may hold values from -6 to 6
- courant_x: float32 [16, 512, 768], P(None, ('group', 'tile')), may hold values from 0.05 to 0.5
- courant_y: float32 [16, 512, 768], P(None, ('group', 'tile')), may hold values from 0.05 to 0.5
- mixing: float32 [15, 512, 768], P(None, ('group', 'tile')), may hold values from 0.02 to 0.3
- snd_column: int32 [32, 8, 128], P(('group', 'tile')), may hold values from 0 to 12287
- snd_count: int32 [32, 8], P(('group', 'tile')), may hold values from 32 to 128, as said below
- snd_step: int32 [32, 8, 128], P(('group', 'tile')), may hold values from 0 to 1
- snd_value: float32 [32, 8, 128], P(('group', 'tile')), may hold values from -6 to 6
- snd_weight: float32 [32, 8, 128], P(('group', 'tile')), may hold values from 0.3 to 3
- snd_kernel: float32 [32, 8, 16, 128], P(('group', 'tile')), may hold values from 0 to 0.5
Outputs:
- adjoint_out: float32 [16, 512, 768], P(None, ('group', 'tile'))
The draws below stay inside these ranges and needn't reach their ends.
Inputs may be any that keep to these rules, and one draw needn't show every extreme that they name: `snd_count`: at most 128; in every draw some destination tile receives 128 soundings from every source device of each group, and every source device fills all slots of some destination tile.
All inputs are finite; a program needn't handle non-finite values.
Results may differ from the reference program's by a relative error of at most 0.0001.
Values sent between devices are 32-bit elements; how exact they have to be, the bound alone decides.
A program may use at most 64 MiB of HBM per device.

```python
import math
import jax
import jax.numpy as jnp
from jax import lax

LEV = 16
CX = 16
CY = 768
CAP = 128
STEPS = 2
NX = 512
N_GROUP = 4
N_TILE = 8


def draw_snd_count(key, part):
    key_base, key_crowd, key_chosen, key_forced = jax.random.split(jax.random.fold_in(key, 17), 4)
    device_total = N_GROUP * N_TILE
    drawn = jax.random.randint(key_base, (device_total, N_TILE), CAP // 4, CAP // 2 + 1)
    tiles = jnp.arange(N_TILE, dtype=jnp.int32)
    crowded = jax.random.randint(key_crowd, (N_TILE,), 0, 6) == 0
    chosen = jax.random.randint(key_chosen, (), 0, N_TILE)
    crowded = crowded | (tiles == chosen)
    forced = jax.random.randint(key_forced, (device_total,), 0, N_TILE)
    filled = crowded[None, :] | (tiles[None, :] == forced[:, None])
    return jnp.where(filled, CAP, drawn).astype(jnp.int32)


def touch_ends(result, stream_key, smallest, top_value):
    extent = result.shape
    index_at = [jax.random.randint(jax.random.fold_in(stream_key, axis), (), 0, extent[axis]) for axis in range(len(extent))]
    result = result.at[tuple(index_at)].set(smallest)
    longest = extent.index(max(extent))
    index_at[longest] = (index_at[longest] + 1) % extent[longest]
    return result.at[tuple(index_at)].set(top_value)


def level_of(rng, dims, cuts, low, high):
    def one(axis_at, parts):
        heights = jax.random.uniform(jax.random.fold_in(jax.random.fold_in(rng, 6), axis_at), (parts,), jnp.float32, low / len(cuts), high / len(cuts))
        return jnp.repeat(jnp.exp(heights), dims[axis_at] // parts).reshape((-1,) + (1,) * (len(dims) - axis_at - 1))

    gain = one(*cuts[0])
    for cut in cuts[1:]:
        gain = gain * one(*cut)
    return gain


def centred(key, dims, scale, bound, shards=(), kind=jnp.bfloat16):
    result = scale * jax.random.normal(key, dims, jnp.float32)
    if shards:
        result = result * level_of(key, dims, shards, -0.22, 0.18)
    return jnp.clip(result, -bound, bound).astype(kind)


def setup_inputs(seed: int = 0) -> dict:
    key_list = jax.random.split(jax.random.key(seed), 12)
    return {
        "checkpoint": centred(key_list[0], (LEV, NX, CY), 1.0, 6.0, ((1, 32),), jnp.float32),
        "adjoint_in": centred(key_list[1], (LEV, NX, CY), 1.0, 6.0, ((1, 32),), jnp.float32),
        "courant_x": jnp.clip(jnp.exp(math.log(0.5) - 2.3025851 * jax.random.uniform(key_list[2], (LEV, NX, CY), jnp.float32) ** level_of(key_list[2], (LEV, NX, CY), ((1, 32),), -0.2, 0.2)), 0.05, 0.5),
        "courant_y": jnp.clip(jnp.exp(math.log(0.5) - 2.3025851 * jax.random.uniform(key_list[3], (LEV, NX, CY), jnp.float32) ** level_of(key_list[3], (LEV, NX, CY), ((1, 32),), -0.2, 0.2)), 0.05, 0.5),
        "mixing": jnp.clip(jnp.exp(math.log(0.3) - 2.7080503 * jax.random.uniform(key_list[4], (LEV - 1, NX, CY), jnp.float32) ** level_of(key_list[4], (LEV - 1, NX, CY), ((1, 32),), -0.2, 0.2)), 0.02, 0.3),
        "snd_column": touch_ends(jax.random.randint(key_list[5], (N_GROUP * N_TILE, N_TILE, CAP), 0, CX * CY), jax.random.fold_in(key_list[5], 1), 0, (CX * CY) - 1).astype(jnp.int32),
        "snd_count": draw_snd_count(jax.random.fold_in(key_list[11], 71), 0),
        "snd_step": touch_ends(jax.random.randint(key_list[7], (N_GROUP * N_TILE, N_TILE, CAP), 0, STEPS), jax.random.fold_in(key_list[7], 1), 0, STEPS - 1).astype(jnp.int32),
        "snd_value": centred(key_list[8], (N_GROUP * N_TILE, N_TILE, CAP), 1.0, 6.0, ((0, 32),), jnp.float32),
        "snd_weight": jnp.clip(jnp.exp(math.log(3.0) - 2.3025851 * jax.random.uniform(key_list[9], (N_GROUP * N_TILE, N_TILE, CAP), jnp.float32) ** level_of(key_list[9], (N_GROUP * N_TILE, N_TILE, CAP), ((0, 32),), -0.2, 0.2)), 0.3, 3.0),
        "snd_kernel": jnp.clip(0.5 * jax.random.uniform(key_list[10], (N_GROUP * N_TILE, N_TILE, LEV, CAP), jnp.float32) ** level_of(key_list[10], (N_GROUP * N_TILE, N_TILE, LEV, CAP), ((0, 32),), -0.2, 0.2), 0.0, 0.5),
    }


def pad_periodic(field, width, along):
    total = field.shape[along]
    return jnp.concatenate([lax.slice_in_dim(field, total - width, total, axis=along), field, lax.slice_in_dim(field, 0, width, axis=along)], axis=along)


def sweep_forward(padded, courant_pad, along):
    interior = padded.shape[along] - 4

    def piece_of(first, last):
        return lax.slice_in_dim(padded, first, last, axis=along)

    courant_face = lax.slice_in_dim(courant_pad, 0, interior + 1, axis=along)
    fluxes = courant_face * (2.0 * piece_of(2, interior + 3) + 5.0 * piece_of(1, interior + 2) - piece_of(0, interior + 1)) / 6.0
    return piece_of(2, interior + 2) + lax.slice_in_dim(fluxes, 0, interior, axis=along) - lax.slice_in_dim(fluxes, 1, interior + 1, axis=along)


def sweep_adjoint(padded, courant_pad, along):
    interior = padded.shape[along] - 4

    def piece_of(first, last):
        return lax.slice_in_dim(padded, first, last, axis=along)

    differences = piece_of(2, interior + 4) - piece_of(1, interior + 3)
    scaled = courant_pad * differences
    return piece_of(2, interior + 2) + (2.0 * lax.slice_in_dim(scaled, 0, interior, axis=along) + 5.0 * lax.slice_in_dim(scaled, 1, interior + 1, axis=along) - lax.slice_in_dim(scaled, 2, interior + 2, axis=along)) / 6.0


def vertical_mix(field, mixing):
    fluxes = mixing * (field[1:] - field[:-1])
    zero_row = jnp.zeros_like(field[:1])
    return field + jnp.concatenate([fluxes, zero_row], axis=0) - jnp.concatenate([zero_row, fluxes], axis=0)


def horizontal(rimmed, wind_x, wind_y):
    swept = sweep_forward(rimmed, wind_x, 1)
    return sweep_forward(pad_periodic(swept, 2, 2), wind_y, 2)


def reference(checkpoint, adjoint_in, courant_x, courant_y, mixing, snd_column, snd_count, snd_step, snd_value, snd_weight, snd_kernel):
    device_total = N_GROUP * N_TILE
    wind_x = pad_periodic(courant_x, 1, 1)
    wind_y = pad_periodic(courant_y, 1, 2)
    tracer = jnp.roll(checkpoint, N_TILE * CX, axis=1)
    states = []
    for moment in range(STEPS):
        tracer = vertical_mix(horizontal(pad_periodic(tracer, 2, 1), wind_x, wind_y), mixing)
        states.append(tracer)
    shape_slots = (device_total, N_TILE, CAP)
    position = lax.broadcasted_iota(jnp.int32, shape_slots, 2)
    source_dev = lax.broadcasted_iota(jnp.int32, shape_slots, 0)
    target_tile = lax.broadcasted_iota(jnp.int32, shape_slots, 1)
    owner_dev = (source_dev // N_TILE) * N_TILE + target_tile
    cell_index = (owner_dev * (CX * CY) + snd_column).astype(jnp.int32).reshape(-1)
    weight = jnp.where(position < snd_count[:, :, None], snd_weight, jnp.zeros_like(snd_weight))
    kernels = snd_kernel.astype(jnp.float32)
    forcings = []
    for moment in range(STEPS):
        flattened = states[moment].reshape(LEV, -1)
        picked = jnp.take(flattened, cell_index, axis=1).reshape(LEV, device_total, N_TILE, CAP)
        observed = jnp.einsum("ldtc,dtlc->dtc", picked, kernels, precision=lax.Precision.HIGHEST)
        misfit = jnp.where(snd_step == moment, weight * (observed - snd_value), jnp.zeros_like(observed))
        contribution = jnp.einsum("dtlc,dtc->ldtc", kernels, misfit, precision=lax.Precision.HIGHEST).reshape(LEV, -1)
        forcing = jnp.zeros((LEV, NX * CY), jnp.float32).at[:, cell_index].add(contribution)
        forcings.append(forcing.reshape(LEV, NX, CY))
    adjoint = adjoint_in
    for moment in reversed(range(STEPS)):
        adjoint = vertical_mix(adjoint + forcings[moment], mixing)
        adjoint = sweep_adjoint(pad_periodic(adjoint, 2, 2), wind_y, 2)
        adjoint = sweep_adjoint(pad_periodic(adjoint, 2, 1), wind_x, 1)
    return adjoint
```

```python
import functools

import jax
import jax.numpy as jnp
from jax import lax
from jax.experimental import pallas as pl
from jax.experimental.pallas import tpu as pltpu
from jax.sharding import PartitionSpec as P

STEPS = 2
MESH = pl.DeviceIdType.MESH
ANY = pl.ANY
LANES = 128
SIXTH = 1.0 / 6.0


def split_parts(v):
    high = v.astype(jnp.bfloat16)
    low = (v - high.astype(jnp.float32)).astype(jnp.bfloat16)
    return high, low


def kernel(
    groups,
    tiles,
    levels,
    wide,
    long,
    cap,
    per,
    chk_in,
    adj_in,
    cx_in,
    cy_in,
    mix_in,
    col_in,
    count_in,
    step_in,
    value_in,
    weight_in,
    kern_in,
    out,
    own,
    landed,
    adj,
    cxl,
    cy,
    mix,
    stage,
    cx,
    t0,
    t1,
    b1,
    b0,
    force,
    parts,
    onehot,
    kern,
    small,
    pack,
    misfit,
    made,
    load_sem,
    send_sem,
    recv_sem,
    snd_send,
    snd_recv,
):
    total = groups * tiles
    g = lax.axis_index("group")
    t = lax.axis_index("tile")
    me = g * tiles + t
    chunks = tiles // per
    width = per * cap

    def flat(offset):
        f = lax.rem(me + offset + total, total)
        return (lax.div(f, tiles), lax.rem(f, tiles))

    def partner(k):
        return (g, lax.rem(t + k, tiles))

    bands = long // LANES
    loads = []
    for k, (src, dst) in enumerate(
        ((chk_in, own), (cx_in, cxl), (cy_in, cy), (mix_in, mix), (adj_in, adj))
    ):
        rows = src.shape[0]
        loads.append(
            [
                pltpu.make_async_copy(
                    src.at[:, pl.ds(j * LANES, LANES)],
                    dst.at[j, pl.ds(0, rows)],
                    load_sem.at[k, j],
                )
                for j in range(bands)
            ]
        )
        for c in loads[-1]:
            c.start()

    def await_all(copies):
        for c in copies:
            c.wait()

    barrier = pltpu.get_barrier_semaphore()
    roles = [flat(o) for o in (1, -1, tiles, tiles + 1, tiles - 1, -tiles, -tiles - 1, 1 - tiles)]
    roles += [partner(k) for k in range(1, tiles)]
    for role in roles:
        pl.semaphore_signal(barrier, inc=1, device_id=role, device_id_type=MESH)

    place = lax.broadcasted_iota(jnp.int32, (1, cap), 1)
    for k in range(tiles):
        pack[k, 0:1, :] = value_in[k : k + 1, :]
        pack[k, 1:2, :] = jnp.where(place < count_in[0, k], weight_in[k : k + 1, :], 0.0)
        pack[k, 2:3, :] = col_in[k : k + 1, :].astype(jnp.float32)
        pack[k, 3:4, :] = step_in[k : k + 1, :].astype(jnp.float32)
    mix[:, pl.ds((levels - 1) * wide, wide), :] = jnp.zeros((bands, wide, LANES), jnp.float32)

    def column(ref, x):
        return jnp.concatenate(
            [ref[j, pl.ds(x, levels, stride=wide), :] for j in range(bands)], axis=1
        )

    pl.semaphore_wait(barrier, len(roles))

    def send(src, dst, k, to):
        c = pltpu.make_async_remote_copy(
            src_ref=src,
            dst_ref=dst,
            send_sem=send_sem.at[k],
            recv_sem=recv_sem.at[k],
            device_id=to,
            device_id_type=MESH,
        )
        c.start()
        return c

    main = [
        send(chk_in.at[:, pl.ds(j * LANES, LANES)], landed.at[j], 11 + j, flat(tiles))
        for j in range(bands)
    ]

    snd = []
    for k in range(1, tiles):
        to = partner(k)
        for j, (src, dst) in enumerate(
            ((kern_in.at[to[1]], kern.at[k]), (pack.at[to[1]], small.at[k]))
        ):
            c = pltpu.make_async_remote_copy(
                src_ref=src,
                dst_ref=dst,
                send_sem=snd_send.at[j, k],
                recv_sem=snd_recv.at[j, k],
                device_id=to,
                device_id_type=MESH,
            )
            c.start()
            snd.append(c)
    for j, (src, dst) in enumerate(((kern_in.at[t], kern.at[0]), (pack.at[t], small.at[0]))):
        c = pltpu.make_async_copy(src, dst, snd_recv.at[j, 0])
        c.start()
        snd.append(c)

    await_all(loads[0])
    stage[0] = column(own, wide - 2)
    stage[1] = column(own, wide - 1)
    stage[2] = column(own, 0)
    rim_low = send(stage.at[pl.ds(0, 2)], t0.at[pl.ds(0, 2)], 1, flat(tiles + 1))
    rim_high = send(stage.at[pl.ds(2, 1)], t0.at[pl.ds(wide + 2, 1)], 2, flat(tiles - 1))
    await_all(loads[1])

    def turn(x, _):
        cx[x + 1] = column(cxl, x) * SIXTH
        return 0

    lax.fori_loop(0, wide, turn, 0)
    wind_low = send(cx.at[pl.ds(wide, 1)], cx.at[pl.ds(0, 1)], 3, flat(1))
    wind_high = send(cx.at[pl.ds(1, 1)], cx.at[pl.ds(wide + 1, 1)], 4, flat(-1))

    for c in snd:
        c.wait()

    def row_of(c, r):
        return jnp.concatenate([small[c * per + k, r : r + 1, :] for k in range(per)], axis=1)

    def kern_of(c):
        return jnp.concatenate([kern[c * per + k] for k in range(per)], axis=1)

    def cell_of(c):
        cell = row_of(c, 2).astype(jnp.int32)
        cx_of = jnp.zeros_like(cell)
        for x in range(1, wide):
            cx_of = cx_of + jnp.where(cell >= x * long, 1, 0)
        return cx_of, cell - cx_of * long

    def mark(c, _):
        _, cy_of = cell_of(c)
        rows = 128
        for first in range(0, long, rows):
            at = lax.broadcasted_iota(jnp.int32, (rows, width), 0) + first
            onehot[c, first : first + rows, :] = jnp.where(at == cy_of, 1.0, 0.0).astype(
                jnp.bfloat16
            )
        return 0

    lax.fori_loop(0, chunks, mark, 0)

    def mixed(v, m):
        f = m * (pltpu.roll(v, levels - 1, 0) - v)
        return v + f - pltpu.roll(f, 1, 0)

    def along_y(v, c):
        f = (c * SIXTH) * (2.0 * pltpu.roll(v, long - 1, 1) + 5.0 * v - pltpu.roll(v, 1, 1))
        return v + pltpu.roll(f, 1, 1) - f

    def back_y(a, c):
        q = (c * SIXTH) * (pltpu.roll(a, long - 1, 1) - a)
        return a + 2.0 * pltpu.roll(q, 1, 1) + 5.0 * q - pltpu.roll(q, long - 1, 1)

    def forward(src, dst):
        def row(x, _):
            before = cx[x] * (2.0 * src[x + 2] + 5.0 * src[x + 1] - src[x])
            after = cx[x + 1] * (2.0 * src[x + 3] + 5.0 * src[x + 2] - src[x + 1])
            v = src[x + 2] + before - after
            v = mixed(along_y(v, column(cy, x)), column(mix, x))
            if dst is not None:
                dst[x + 2] = v
            high, low = split_parts(v)
            at = pl.multiple_of(x * 2 * levels, 2 * levels)
            parts[pl.ds(at, levels), :] = high
            parts[pl.ds(at + levels, levels), :] = low
            return 0

        return row

    def observe(moment):
        def one(c, _):
            picked = jnp.dot(parts[...], onehot[c], preferred_element_type=jnp.float32)
            cx_of, _ = cell_of(c)
            seen = jnp.zeros((2 * levels, width), jnp.float32)
            for x in range(wide):
                seen = seen + jnp.where(
                    cx_of == x, picked[x * 2 * levels : (x + 1) * 2 * levels], 0.0
                )
            seen = seen[:levels] + seen[levels:]
            seen = jnp.sum(seen * kern_of(c), axis=0, keepdims=True)
            gap = row_of(c, 1) * (seen - row_of(c, 0))
            misfit[c, moment : moment + 1, :] = jnp.where(
                row_of(c, 3).astype(jnp.int32) == moment, gap, 0.0
            )
            return 0

        lax.fori_loop(0, chunks, one, 0)

    def spread(moment):
        force[...] = jnp.zeros_like(force)

        def one(c, _):
            high, low = split_parts(kern_of(c) * misfit[c, moment : moment + 1, :])
            high, low = high.astype(jnp.float32), low.astype(jnp.float32)
            cx_of, _ = cell_of(c)
            rows = []
            for part in (high, low):
                for x in range(wide):
                    rows.append(jnp.where(cx_of == x, part, 0.0).astype(jnp.bfloat16))
            sums = lax.dot_general(
                jnp.concatenate(rows, axis=0),
                onehot[c],
                (((1,), (1,)), ((), ())),
                preferred_element_type=jnp.float32,
            )
            half = wide * levels
            force[...] += sums[:half] + sums[half:]
            return 0

        lax.fori_loop(0, chunks, one, 0)

    def force_at(x):
        return force[pl.ds(pl.multiple_of(x * levels, levels), levels), :]

    await_all(main)

    def place_row(x, _):
        t0[x + 2] = column(landed, x)
        return 0

    lax.fori_loop(0, wide, place_row, 0)
    await_all(loads[2])
    await_all(loads[3])
    for c in (rim_low, rim_high, wind_low, wind_high):
        c.wait()
    row = forward(t0, t1)
    for x in (0, wide - 2, wide - 1):
        row(x, 0)
    low1 = send(t1.at[pl.ds(wide, 2)], t1.at[pl.ds(0, 2)], 5, flat(1))
    high1 = send(t1.at[pl.ds(2, 1)], t1.at[pl.ds(wide + 2, 1)], 6, flat(-1))
    lax.fori_loop(1, wide - 2, row, 0)
    observe(0)
    low1.wait()
    high1.wait()
    lax.fori_loop(0, wide, forward(t1, None), 0)
    observe(1)

    await_all(loads[4])
    spread(1)

    def first_back(x, _):
        a = mixed(column(adj, x) + force_at(x), column(mix, x))
        b1[x + 2] = back_y(a, column(cy, x))
        return 0

    def back_x(src, x):
        d0 = src[x + 2]
        d1 = src[x + 3]
        q_before = cx[x] * (d0 - src[x + 1])
        q_here = cx[x + 1] * (d1 - d0)
        q_after = cx[x + 2] * (src[x + 4] - d1)
        return d0 + 2.0 * q_before + 5.0 * q_here - q_after

    def rims_back(buf, k):
        return (
            send(buf.at[pl.ds(wide + 1, 1)], buf.at[pl.ds(1, 1)], k, flat(1)),
            send(buf.at[pl.ds(2, 2)], buf.at[pl.ds(wide + 2, 2)], k + 1, flat(-1)),
        )

    for x in (0, 1, wide - 1):
        first_back(x, 0)
    rims = rims_back(b1, 7)
    lax.fori_loop(2, wide - 1, first_back, 0)
    spread(0)
    for c in rims:
        c.wait()

    def second_back(x, _):
        a = mixed(back_x(b1, x) + force_at(x), column(mix, x))
        b0[x + 2] = back_y(a, column(cy, x))
        return 0

    for x in (0, 1, wide - 1):
        second_back(x, 0)
    rims = rims_back(b0, 9)
    lax.fori_loop(2, wide - 1, second_back, 0)

    def last(x, _):
        v = back_x(b0, x)
        for j in range(bands):
            made[j, pl.ds(x, levels, stride=wide), :] = v[:, j * LANES : (j + 1) * LANES]
        return 0

    lax.fori_loop(1, wide - 2, last, 0)
    for c in rims:
        c.wait()
    for x in (0, wide - 2, wide - 1):
        last(x, 0)
    stores = [
        pltpu.make_async_copy(
            made.at[j], out.at[:, pl.ds(j * LANES, LANES)], load_sem.at[5, j]
        )
        for j in range(bands)
    ]
    for c in stores:
        c.start()
    await_all(stores)


def on_device(
    groups,
    tiles,
    checkpoint,
    adjoint_in,
    courant_x,
    courant_y,
    mixing,
    snd_column,
    snd_count,
    snd_step,
    snd_value,
    snd_weight,
    snd_kernel,
):
    levels, wide, long = checkpoint.shape
    cap = snd_column.shape[2]
    per = 2 if tiles % 2 == 0 else 1
    f32 = jnp.float32
    plane = (levels * wide, long)
    bands = long // LANES
    banded = (bands, levels * wide, LANES)
    rimmed = (wide + 4, levels, long)
    vmem = pl.BlockSpec(memory_space=pltpu.VMEM)
    smem = pl.BlockSpec(memory_space=pltpu.SMEM)
    anywhere = pl.BlockSpec(memory_space=ANY)
    result = pl.pallas_call(
        functools.partial(kernel, groups, tiles, levels, wide, long, cap, per),
        out_shape=jax.ShapeDtypeStruct(plane, f32),
        in_specs=[anywhere] * 5 + [vmem, smem, vmem, vmem, vmem, anywhere],
        out_specs=anywhere,
        scratch_shapes=[
            pltpu.VMEM(banded, f32),
            pltpu.VMEM(banded, f32),
            pltpu.VMEM(banded, f32),
            pltpu.VMEM(banded, f32),
            pltpu.VMEM(banded, f32),
            pltpu.VMEM(banded, f32),
            pltpu.VMEM((3, levels, long), f32),
            pltpu.VMEM((wide + 2, levels, long), f32),
            pltpu.VMEM(rimmed, f32),
            pltpu.VMEM(rimmed, f32),
            pltpu.VMEM(rimmed, f32),
            pltpu.VMEM(rimmed, f32),
            pltpu.VMEM(plane, f32),
            pltpu.VMEM((2 * levels * wide, long), jnp.bfloat16),
            pltpu.VMEM((tiles // per, long, per * cap), jnp.bfloat16),
            pltpu.VMEM((tiles, levels, cap), f32),
            pltpu.VMEM((tiles, 8, cap), f32),
            pltpu.VMEM((tiles, 8, cap), f32),
            pltpu.VMEM((tiles // per, 8, per * cap), f32),
            pltpu.VMEM(banded, f32),
            pltpu.SemaphoreType.DMA((6, bands)),
            pltpu.SemaphoreType.DMA((11 + bands,)),
            pltpu.SemaphoreType.DMA((11 + bands,)),
            pltpu.SemaphoreType.DMA((2, tiles)),
            pltpu.SemaphoreType.DMA((2, tiles)),
        ],
        compiler_params=pltpu.CompilerParams(
            collective_id=0, has_side_effects=True, vmem_limit_bytes=48 * 1024 * 1024
        ),
        name="window",
    )(
        checkpoint.reshape(plane),
        adjoint_in.reshape(plane),
        courant_x.reshape(plane),
        courant_y.reshape(plane),
        mixing.reshape(-1, long),
        snd_column.reshape(tiles, cap),
        snd_count,
        snd_step.reshape(tiles, cap),
        snd_value.reshape(tiles, cap),
        snd_weight.reshape(tiles, cap),
        snd_kernel.reshape(tiles, levels, cap),
    )
    return result.reshape(checkpoint.shape)


def solution(mesh):
    return jax.shard_map(
        functools.partial(on_device, mesh.shape["group"], mesh.shape["tile"]),
        mesh=mesh,
        in_specs=(
            P(None, ("group", "tile"), None),
            P(None, ("group", "tile"), None),
            P(None, ("group", "tile"), None),
            P(None, ("group", "tile"), None),
            P(None, ("group", "tile"), None),
            P(("group", "tile"), None, None),
            P(("group", "tile"), None),
            P(("group", "tile"), None, None),
            P(("group", "tile"), None, None),
            P(("group", "tile"), None, None),
            P(("group", "tile"), None, None, None),
        ),
        out_specs=P(None, ("group", "tile"), None),
        check_vma=False,
    )
```

```python
import functools

import jax
import jax.numpy as jnp
from jax import lax
from jax.experimental import pallas as pl
from jax.experimental.pallas import tpu as pltpu
from jax.sharding import PartitionSpec as P

STEPS = 2
MESH = pl.DeviceIdType.MESH
ANY = pltpu.HBM
LANES = 128
SIXTH = 1.0 / 6.0


def split_parts(v):
    high = v.astype(jnp.bfloat16)
    low = (v - high.astype(jnp.float32)).astype(jnp.bfloat16)
    return high, low


def kernel(
    groups,
    tiles,
    levels,
    wide,
    long,
    cap,
    per,
    chk_in,
    adj_in,
    cx_in,
    cy_in,
    mix_in,
    col_in,
    count_in,
    step_in,
    value_in,
    weight_in,
    kern_in,
    out,
    own,
    landed,
    adj,
    cxl,
    cy,
    mix,
    stage,
    cx,
    t0,
    t1,
    b1,
    b0,
    force,
    parts,
    onehot,
    kern,
    small,
    pack,
    misfit,
    made,
    col,
    count,
    step,
    value,
    weight,
    light_sem,
    load_sem,
    send_sem,
    recv_sem,
    snd_send,
    snd_recv,
):
    total = groups * tiles
    g = lax.axis_index("group")
    t = lax.axis_index("tile")
    me = g * tiles + t
    chunks = tiles // per
    width = per * cap

    def flat(offset):
        f = lax.rem(me + offset + total, total)
        return (lax.div(f, tiles), lax.rem(f, tiles))

    def partner(k):
        return (g, lax.rem(t + k, tiles))

    light = [
        pltpu.make_async_copy(src, dst, light_sem.at[k])
        for k, (src, dst) in enumerate(
            (
                (col_in, col),
                (count_in, count),
                (step_in, step),
                (value_in, value),
                (weight_in, weight),
            )
        )
    ]
    for c in light:
        c.start()
    bands = long // LANES
    loads = []
    for k, (src, dst) in enumerate(
        ((chk_in, own), (cx_in, cxl), (cy_in, cy), (mix_in, mix), (adj_in, adj))
    ):
        rows = src.shape[0]
        loads.append(
            [
                pltpu.make_async_copy(
                    src.at[:, pl.ds(j * LANES, LANES)],
                    dst.at[j, pl.ds(0, rows)],
                    load_sem.at[k, j],
                )
                for j in range(bands)
            ]
        )
        for c in loads[-1]:
            c.start()

    def await_all(copies):
        for c in copies:
            c.wait()

    barrier = pltpu.get_barrier_semaphore()
    roles = [flat(o) for o in (1, -1, tiles, tiles + 1, tiles - 1, -tiles, -tiles - 1, 1 - tiles)]
    roles += [partner(k) for k in range(1, tiles)]
    for role in roles:
        pl.semaphore_signal(barrier, inc=1, device_id=role, device_id_type=MESH)

    await_all(light)
    place = lax.broadcasted_iota(jnp.int32, (1, cap), 1)
    for k in range(tiles):
        pack[k, 0:1, :] = value[k : k + 1, :]
        pack[k, 1:2, :] = jnp.where(place < count[0, k], weight[k : k + 1, :], 0.0)
        pack[k, 2:3, :] = col[k : k + 1, :].astype(jnp.float32)
        pack[k, 3:4, :] = step[k : k + 1, :].astype(jnp.float32)
    mix[:, pl.ds((levels - 1) * wide, wide), :] = jnp.zeros((bands, wide, LANES), jnp.float32)

    def column(ref, x):
        return jnp.concatenate(
            [ref[j, pl.ds(x, levels, stride=wide), :] for j in range(bands)], axis=1
        )

    pl.semaphore_wait(barrier, len(roles))

    def send(src, dst, k, to):
        c = pltpu.make_async_remote_copy(
            src_ref=src,
            dst_ref=dst,
            send_sem=send_sem.at[k],
            recv_sem=recv_sem.at[k],
            device_id=to,
            device_id_type=MESH,
        )
        c.start()
        return c

    main = [
        send(chk_in.at[:, pl.ds(j * LANES, LANES)], landed.at[j], 11 + j, flat(tiles))
        for j in range(bands)
    ]

    snd = []
    for k in range(1, tiles):
        to = partner(k)
        for j, (src, dst) in enumerate(
            ((kern_in.at[to[1]], kern.at[k]), (pack.at[to[1]], small.at[k]))
        ):
            c = pltpu.make_async_remote_copy(
                src_ref=src,
                dst_ref=dst,
                send_sem=snd_send.at[j, k],
                recv_sem=snd_recv.at[j, k],
                device_id=to,
                device_id_type=MESH,
            )
            c.start()
            snd.append(c)
    for j, (src, dst) in enumerate(((kern_in.at[t], kern.at[0]), (pack.at[t], small.at[0]))):
        c = pltpu.make_async_copy(src, dst, snd_recv.at[j, 0])
        c.start()
        snd.append(c)

    await_all(loads[0])
    stage[0] = column(own, wide - 2)
    stage[1] = column(own, wide - 1)
    stage[2] = column(own, 0)
    rim_low = send(stage.at[pl.ds(0, 2)], t0.at[pl.ds(0, 2)], 1, flat(tiles + 1))
    rim_high = send(stage.at[pl.ds(2, 1)], t0.at[pl.ds(wide + 2, 1)], 2, flat(tiles - 1))
    await_all(loads[1])

    def turn(x, _):
        cx[x + 1] = column(cxl, x) * SIXTH
        return 0

    lax.fori_loop(0, wide, turn, 0)
    wind_low = send(cx.at[pl.ds(wide, 1)], cx.at[pl.ds(0, 1)], 3, flat(1))
    wind_high = send(cx.at[pl.ds(1, 1)], cx.at[pl.ds(wide + 1, 1)], 4, flat(-1))

    for c in snd:
        c.wait()

    def row_of(c, r):
        return jnp.concatenate([small[c * per + k, r : r + 1, :] for k in range(per)], axis=1)

    def kern_of(c):
        return jnp.concatenate([kern[c * per + k] for k in range(per)], axis=1)

    def cell_of(c):
        cell = row_of(c, 2).astype(jnp.int32)
        cx_of = jnp.zeros_like(cell)
        for x in range(1, wide):
            cx_of = cx_of + jnp.where(cell >= x * long, 1, 0)
        return cx_of, cell - cx_of * long

    def mark(c, _):
        _, cy_of = cell_of(c)
        rows = 128
        for first in range(0, long, rows):
            at = lax.broadcasted_iota(jnp.int32, (rows, width), 0) + first
            onehot[c, first : first + rows, :] = jnp.where(at == cy_of, 1.0, 0.0).astype(
                jnp.bfloat16
            )
        return 0

    lax.fori_loop(0, chunks, mark, 0)

    def mixed(v, m):
        f = m * (pltpu.roll(v, levels - 1, 0) - v)
        return v + f - pltpu.roll(f, 1, 0)

    def along_y(v, c):
        f = (c * SIXTH) * (2.0 * pltpu.roll(v, long - 1, 1) + 5.0 * v - pltpu.roll(v, 1, 1))
        return v + pltpu.roll(f, 1, 1) - f

    def back_y(a, c):
        q = (c * SIXTH) * (pltpu.roll(a, long - 1, 1) - a)
        return a + 2.0 * pltpu.roll(q, 1, 1) + 5.0 * q - pltpu.roll(q, long - 1, 1)

    def forward(src, dst):
        def row(x, _):
            before = cx[x] * (2.0 * src[x + 2] + 5.0 * src[x + 1] - src[x])
            after = cx[x + 1] * (2.0 * src[x + 3] + 5.0 * src[x + 2] - src[x + 1])
            v = src[x + 2] + before - after
            v = mixed(along_y(v, column(cy, x)), column(mix, x))
            if dst is not None:
                dst[x + 2] = v
            high, low = split_parts(v)
            at = pl.multiple_of(x * 2 * levels, 2 * levels)
            parts[pl.ds(at, levels), :] = high
            parts[pl.ds(at + levels, levels), :] = low
            return 0

        return row

    def observe(moment):
        def one(c, _):
            picked = jnp.dot(parts[...], onehot[c], preferred_element_type=jnp.float32)
            cx_of, _ = cell_of(c)
            seen = jnp.zeros((2 * levels, width), jnp.float32)
            for x in range(wide):
                seen = seen + jnp.where(
                    cx_of == x, picked[x * 2 * levels : (x + 1) * 2 * levels], 0.0
                )
            seen = seen[:levels] + seen[levels:]
            seen = jnp.sum(seen * kern_of(c), axis=0, keepdims=True)
            gap = row_of(c, 1) * (seen - row_of(c, 0))
            misfit[c, moment : moment + 1, :] = jnp.where(
                row_of(c, 3).astype(jnp.int32) == moment, gap, 0.0
            )
            return 0

        lax.fori_loop(0, chunks, one, 0)

    def spread(moment):
        force[...] = jnp.zeros_like(force)

        def one(c, _):
            high, low = split_parts(kern_of(c) * misfit[c, moment : moment + 1, :])
            high, low = high.astype(jnp.float32), low.astype(jnp.float32)
            cx_of, _ = cell_of(c)
            rows = []
            for part in (high, low):
                for x in range(wide):
                    rows.append(jnp.where(cx_of == x, part, 0.0).astype(jnp.bfloat16))
            sums = lax.dot_general(
                jnp.concatenate(rows, axis=0),
                onehot[c],
                (((1,), (1,)), ((), ())),
                preferred_element_type=jnp.float32,
            )
            half = wide * levels
            force[...] += sums[:half] + sums[half:]
            return 0

        lax.fori_loop(0, chunks, one, 0)

    def force_at(x):
        return force[pl.ds(pl.multiple_of(x * levels, levels), levels), :]

    await_all(main)

    def place_row(x, _):
        t0[x + 2] = column(landed, x)
        return 0

    lax.fori_loop(0, wide, place_row, 0)
    await_all(loads[2])
    await_all(loads[3])
    for c in (rim_low, rim_high, wind_low, wind_high):
        c.wait()
    row = forward(t0, t1)
    for x in (0, wide - 2, wide - 1):
        row(x, 0)
    low1 = send(t1.at[pl.ds(wide, 2)], t1.at[pl.ds(0, 2)], 5, flat(1))
    high1 = send(t1.at[pl.ds(2, 1)], t1.at[pl.ds(wide + 2, 1)], 6, flat(-1))
    lax.fori_loop(1, wide - 2, row, 0)
    observe(0)
    low1.wait()
    high1.wait()
    lax.fori_loop(0, wide, forward(t1, None), 0)
    observe(1)

    await_all(loads[4])
    spread(1)

    def first_back(x, _):
        a = mixed(column(adj, x) + force_at(x), column(mix, x))
        b1[x + 2] = back_y(a, column(cy, x))
        return 0

    def back_x(src, x):
        d0 = src[x + 2]
        d1 = src[x + 3]
        q_before = cx[x] * (d0 - src[x + 1])
        q_here = cx[x + 1] * (d1 - d0)
        q_after = cx[x + 2] * (src[x + 4] - d1)
        return d0 + 2.0 * q_before + 5.0 * q_here - q_after

    def rims_back(buf, k):
        return (
            send(buf.at[pl.ds(wide + 1, 1)], buf.at[pl.ds(1, 1)], k, flat(1)),
            send(buf.at[pl.ds(2, 2)], buf.at[pl.ds(wide + 2, 2)], k + 1, flat(-1)),
        )

    for x in (0, 1, wide - 1):
        first_back(x, 0)
    rims = rims_back(b1, 7)
    lax.fori_loop(2, wide - 1, first_back, 0)
    spread(0)
    for c in rims:
        c.wait()

    def second_back(x, _):
        a = mixed(back_x(b1, x) + force_at(x), column(mix, x))
        b0[x + 2] = back_y(a, column(cy, x))
        return 0

    for x in (0, 1, wide - 1):
        second_back(x, 0)
    rims = rims_back(b0, 9)
    lax.fori_loop(2, wide - 1, second_back, 0)

    def last(x, _):
        v = back_x(b0, x)
        for j in range(bands):
            made[j, pl.ds(x, levels, stride=wide), :] = v[:, j * LANES : (j + 1) * LANES]
        return 0

    lax.fori_loop(1, wide - 2, last, 0)
    for c in rims:
        c.wait()
    for x in (0, wide - 2, wide - 1):
        last(x, 0)
    stores = [
        pltpu.make_async_copy(
            made.at[j], out.at[:, pl.ds(j * LANES, LANES)], load_sem.at[5, j]
        )
        for j in range(bands)
    ]
    for c in stores:
        c.start()
    await_all(stores)


def on_device(
    groups,
    tiles,
    checkpoint,
    adjoint_in,
    courant_x,
    courant_y,
    mixing,
    snd_column,
    snd_count,
    snd_step,
    snd_value,
    snd_weight,
    snd_kernel,
):
    levels, wide, long = checkpoint.shape
    cap = snd_column.shape[2]
    per = 2 if tiles % 2 == 0 else 1
    f32 = jnp.float32
    plane = (levels * wide, long)
    bands = long // LANES
    banded = (bands, levels * wide, LANES)
    rimmed = (wide + 4, levels, long)
    anywhere = pl.BlockSpec(memory_space=ANY)
    result = pl.pallas_call(
        functools.partial(kernel, groups, tiles, levels, wide, long, cap, per),
        out_shape=jax.ShapeDtypeStruct(plane, f32),
        in_specs=[anywhere] * 11,
        out_specs=anywhere,
        scratch_shapes=[
            pltpu.VMEM(banded, f32),
            pltpu.VMEM(banded, f32),
            pltpu.VMEM(banded, f32),
            pltpu.VMEM(banded, f32),
            pltpu.VMEM(banded, f32),
            pltpu.VMEM(banded, f32),
            pltpu.VMEM((3, levels, long), f32),
            pltpu.VMEM((wide + 2, levels, long), f32),
            pltpu.VMEM(rimmed, f32),
            pltpu.VMEM(rimmed, f32),
            pltpu.VMEM(rimmed, f32),
            pltpu.VMEM(rimmed, f32),
            pltpu.VMEM(plane, f32),
            pltpu.VMEM((2 * levels * wide, long), jnp.bfloat16),
            pltpu.VMEM((tiles // per, long, per * cap), jnp.bfloat16),
            pltpu.VMEM((tiles, levels, cap), f32),
            pltpu.VMEM((tiles, 8, cap), f32),
            pltpu.VMEM((tiles, 8, cap), f32),
            pltpu.VMEM((tiles // per, 8, per * cap), f32),
            pltpu.VMEM(banded, f32),
            pltpu.VMEM((tiles, cap), jnp.int32),
            pltpu.SMEM((1, tiles), jnp.int32),
            pltpu.VMEM((tiles, cap), jnp.int32),
            pltpu.VMEM((tiles, cap), f32),
            pltpu.VMEM((tiles, cap), f32),
            pltpu.SemaphoreType.DMA((5,)),
            pltpu.SemaphoreType.DMA((6, bands)),
            pltpu.SemaphoreType.DMA((11 + bands,)),
            pltpu.SemaphoreType.DMA((11 + bands,)),
            pltpu.SemaphoreType.DMA((2, tiles)),
            pltpu.SemaphoreType.DMA((2, tiles)),
        ],
        compiler_params=pltpu.CompilerParams(
            collective_id=0, has_side_effects=True, vmem_limit_bytes=48 * 1024 * 1024
        ),
        name="window",
    )(
        *(
            pltpu.with_memory_space_constraint(v, pltpu.HBM)
            for v in (
                checkpoint.reshape(plane),
                adjoint_in.reshape(plane),
                courant_x.reshape(plane),
                courant_y.reshape(plane),
                mixing.reshape(-1, long),
                snd_column.reshape(tiles, cap),
                snd_count,
                snd_step.reshape(tiles, cap),
                snd_value.reshape(tiles, cap),
                snd_weight.reshape(tiles, cap),
                snd_kernel.reshape(tiles, levels, cap),
            )
        )
    )
    return result.reshape(checkpoint.shape)


def solution(mesh):
    return jax.shard_map(
        functools.partial(on_device, mesh.shape["group"], mesh.shape["tile"]),
        mesh=mesh,
        in_specs=(
            P(None, ("group", "tile"), None),
            P(None, ("group", "tile"), None),
            P(None, ("group", "tile"), None),
            P(None, ("group", "tile"), None),
            P(None, ("group", "tile"), None),
            P(("group", "tile"), None, None),
            P(("group", "tile"), None),
            P(("group", "tile"), None, None),
            P(("group", "tile"), None, None),
            P(("group", "tile"), None, None),
            P(("group", "tile"), None, None, None),
        ),
        out_specs=P(None, ("group", "tile"), None),
        check_vma=False,
    )
```

```python
import functools

import jax
import jax.numpy as jnp
from jax import lax
from jax.experimental import pallas as pl
from jax.experimental.pallas import tpu as pltpu
from jax.sharding import PartitionSpec as P

STEPS = 2
MESH = pl.DeviceIdType.MESH
ANY = pltpu.HBM
LANES = 128
PER = 4
SIXTH = 1.0 / 6.0


def split_parts(v):
    high = v.astype(jnp.bfloat16)
    low = (v - high.astype(jnp.float32)).astype(jnp.bfloat16)
    return high, low


def kernel(
    groups,
    tiles,
    levels,
    wide,
    long,
    cap,
    per,
    chk_in,
    adj_in,
    cx_in,
    cy_in,
    mix_in,
    col_in,
    count_in,
    step_in,
    value_in,
    weight_in,
    kern_in,
    out,
    own,
    landed,
    adj,
    cxl,
    cy,
    mix,
    stage,
    cx,
    t0,
    t1,
    b1,
    b0,
    force,
    parts,
    onehot,
    cyx,
    mixx,
    adjx,
    line,
    lines,
    kern,
    small,
    pack,
    misfit,
    made,
    col,
    count,
    step,
    value,
    weight,
    light_sem,
    load_sem,
    send_sem,
    recv_sem,
    snd_send,
    snd_recv,
):
    total = groups * tiles
    g = lax.axis_index("group")
    t = lax.axis_index("tile")
    me = g * tiles + t
    chunks = tiles // per
    width = per * cap

    def flat(offset):
        f = lax.rem(me + offset + total, total)
        return (lax.div(f, tiles), lax.rem(f, tiles))

    def partner(k):
        return (g, lax.rem(t + k, tiles))

    light = [
        pltpu.make_async_copy(src, dst, light_sem.at[k])
        for k, (src, dst) in enumerate(
            (
                (col_in, col),
                (count_in, count),
                (step_in, step),
                (value_in, value),
                (weight_in, weight),
            )
        )
    ]
    for c in light:
        c.start()
    bands = long // LANES
    loads = []
    for k, (src, dst) in enumerate(
        ((chk_in, own), (cx_in, cxl), (cy_in, cy), (mix_in, mix), (adj_in, adj))
    ):
        rows = src.shape[0]
        loads.append(
            [
                pltpu.make_async_copy(
                    src.at[:, pl.ds(j * LANES, LANES)],
                    dst.at[j, pl.ds(0, rows)],
                    load_sem.at[k, j],
                )
                for j in range(bands)
            ]
        )
        for c in loads[-1]:
            c.start()

    def await_all(copies):
        for c in copies:
            c.wait()

    barrier = pltpu.get_barrier_semaphore()
    roles = [flat(o) for o in (1, -1, tiles, tiles + 1, tiles - 1, -tiles, -tiles - 1, 1 - tiles)]
    roles += [partner(k) for k in range(1, tiles)]
    for role in roles:
        pl.semaphore_signal(barrier, inc=1, device_id=role, device_id_type=MESH)

    await_all(light)
    place = lax.broadcasted_iota(jnp.int32, (1, cap), 1)
    for k in range(tiles):
        pack[k, 0:1, :] = value[k : k + 1, :]
        pack[k, 1:2, :] = jnp.where(place < count[0, k], weight[k : k + 1, :], 0.0)
        pack[k, 2:3, :] = col[k : k + 1, :].astype(jnp.float32)
        pack[k, 3:4, :] = step[k : k + 1, :].astype(jnp.float32)
    mix[:, pl.ds((levels - 1) * wide, wide), :] = jnp.zeros((bands, wide, LANES), jnp.float32)

    def column(ref, x):
        return jnp.concatenate(
            [ref[j, pl.ds(x, levels, stride=wide), :] for j in range(bands)], axis=1
        )

    pl.semaphore_wait(barrier, len(roles))

    def send(src, dst, k, to):
        c = pltpu.make_async_remote_copy(
            src_ref=src,
            dst_ref=dst,
            send_sem=send_sem.at[k],
            recv_sem=recv_sem.at[k],
            device_id=to,
            device_id_type=MESH,
        )
        c.start()
        return c

    main = [
        send(chk_in.at[:, pl.ds(j * LANES, LANES)], landed.at[j], 11 + j, flat(tiles))
        for j in range(bands)
    ]

    snd = []
    for k in range(1, tiles):
        to = partner(k)
        for j, (src, dst) in enumerate(
            ((kern_in.at[to[1]], kern.at[k]), (pack.at[to[1]], small.at[k]))
        ):
            c = pltpu.make_async_remote_copy(
                src_ref=src,
                dst_ref=dst,
                send_sem=snd_send.at[j, k],
                recv_sem=snd_recv.at[j, k],
                device_id=to,
                device_id_type=MESH,
            )
            c.start()
            snd.append(c)
    for j, (src, dst) in enumerate(((kern_in.at[t], kern.at[0]), (pack.at[t], small.at[0]))):
        c = pltpu.make_async_copy(src, dst, snd_recv.at[j, 0])
        c.start()
        snd.append(c)

    await_all(loads[0])
    stage[0] = column(own, wide - 2)
    stage[1] = column(own, wide - 1)
    stage[2] = column(own, 0)
    rim_low = send(stage.at[pl.ds(0, 2)], t0.at[pl.ds(0, 2)], 1, flat(tiles + 1))
    rim_high = send(stage.at[pl.ds(2, 1)], t0.at[pl.ds(wide + 2, 1)], 2, flat(tiles - 1))
    await_all(loads[1])

    def turn(x, _):
        cx[x + 1] = column(cxl, x) * SIXTH
        return 0

    def turn_rest(x, _):
        cyx[x] = column(cy, x) * SIXTH
        mixx[x] = column(mix, x)
        adjx[x] = column(adj, x)
        return 0

    lax.fori_loop(0, wide, turn, 0)
    wind_low = send(cx.at[pl.ds(wide, 1)], cx.at[pl.ds(0, 1)], 3, flat(1))
    wind_high = send(cx.at[pl.ds(1, 1)], cx.at[pl.ds(wide + 1, 1)], 4, flat(-1))

    for c in snd:
        c.wait()

    def row_of(c, r):
        return jnp.concatenate([small[c * per + k, r : r + 1, :] for k in range(per)], axis=1)

    def kern_of(c):
        return jnp.concatenate([kern[c * per + k] for k in range(per)], axis=1)

    def cell_of(c):
        cell = row_of(c, 2).astype(jnp.int32)
        cx_of = jnp.zeros_like(cell)
        for x in range(1, wide):
            cx_of = cx_of + jnp.where(cell >= x * long, 1, 0)
        return cx_of, cell - cx_of * long

    def mark(c, _):
        _, cy_of = cell_of(c)
        rows = 128
        for first in range(0, long, rows):
            at = lax.broadcasted_iota(jnp.int32, (rows, width), 0) + first
            onehot[c, first : first + rows, :] = jnp.where(at == cy_of, 1.0, 0.0).astype(
                jnp.bfloat16
            )
        return 0

    lax.fori_loop(0, chunks, mark, 0)

    lane = lax.broadcasted_iota(jnp.int32, (levels, LANES), 1)
    at_first = lane == 0
    at_last = lane == LANES - 1

    def get(ref, x):
        return [ref[x, :, j * LANES : (j + 1) * LANES] for j in range(bands)]

    def put(ref, x, v):
        for j in range(bands):
            ref[x, :, j * LANES : (j + 1) * LANES] = v[j]

    def each(f, *lists):
        return [f(*items) for items in zip(*lists)]

    def ahead(v):
        r = [pltpu.roll(b, LANES - 1, 1) for b in v]
        return [jnp.where(at_last, r[(j + 1) % bands], r[j]) for j in range(bands)]

    def behind(v):
        r = [pltpu.roll(b, 1, 1) for b in v]
        return [jnp.where(at_first, r[j - 1], r[j]) for j in range(bands)]

    def mixed(v, m):
        f = m * (pltpu.roll(v, levels - 1, 0) - v)
        return v + f - pltpu.roll(f, 1, 0)

    def flux(c, after, here, before):
        return c * (2.0 * after + 5.0 * here - before)

    def gather_back(a, before, here, after):
        return a + 2.0 * before + 5.0 * here - after

    def forward(src, dst):
        def row(x, fresh):
            if fresh:
                lead = each(flux, get(cx, x), get(src, x + 2), get(src, x + 1), get(src, x))
            else:
                lead = get(line, 0)
            here = get(src, x + 2)
            trail = each(flux, get(cx, x + 1), get(src, x + 3), here, get(src, x + 1))
            put(line, 0, trail)
            v = each(lambda p, q, r: p + q - r, here, lead, trail)
            f = each(flux, get(cyx, x), ahead(v), v, behind(v))
            v = each(lambda p, q, r: p + q - r, v, behind(f), f)
            at = pl.multiple_of(x * 2 * levels, 2 * levels)
            for j, (b, m) in enumerate(zip(v, get(mixx, x))):
                b = mixed(b, m)
                across = slice(j * LANES, (j + 1) * LANES)
                if dst is not None:
                    dst[x + 2, :, across] = b
                high, low = split_parts(b)
                parts[pl.ds(at, levels), across] = high
                parts[pl.ds(at + levels, levels), across] = low

        return row

    def run(first, last, row):
        def body(x, _):
            row(x, False)
            return 0

        lax.fori_loop(first, last, body, 0)

    def observe(moment):
        def one(c, _):
            picked = jnp.dot(parts[...], onehot[c], preferred_element_type=jnp.float32)
            cx_of, _ = cell_of(c)
            seen = jnp.zeros((2 * levels, width), jnp.float32)
            for x in range(wide):
                seen = seen + jnp.where(
                    cx_of == x, picked[x * 2 * levels : (x + 1) * 2 * levels], 0.0
                )
            seen = seen[:levels] + seen[levels:]
            seen = jnp.sum(seen * kern_of(c), axis=0, keepdims=True)
            gap = row_of(c, 1) * (seen - row_of(c, 0))
            misfit[c, moment : moment + 1, :] = jnp.where(
                row_of(c, 3).astype(jnp.int32) == moment, gap, 0.0
            )
            return 0

        lax.fori_loop(0, chunks, one, 0)

    def spread(moment):
        def one(c, first):
            high, low = split_parts(kern_of(c) * misfit[c, moment : moment + 1, :])
            high, low = high.astype(jnp.float32), low.astype(jnp.float32)
            cx_of, _ = cell_of(c)
            rows = []
            for x in range(wide):
                for part in (high, low):
                    rows.append(jnp.where(cx_of == x, part, 0.0).astype(jnp.bfloat16))
            sums = lax.dot_general(
                jnp.concatenate(rows, axis=0),
                onehot[c],
                (((1,), (1,)), ((), ())),
                preferred_element_type=jnp.float32,
            )
            for x in range(wide):
                at = 2 * x * levels
                v = sums[at : at + levels] + sums[at + levels : at + 2 * levels]
                force[x] = v if first else force[x] + v

        one(0, True)

        def more(c, _):
            one(c, False)
            return 0

        if chunks > 1:
            lax.fori_loop(1, chunks, more, 0)

    def get_force(x):
        return get(force, x)

    for k in (2, 3, 4):
        await_all(loads[k])
    lax.fori_loop(0, wide, turn_rest, 0)
    await_all(main)

    def place_row(x, _):
        t0[x + 2] = column(landed, x)
        return 0

    lax.fori_loop(0, wide, place_row, 0)
    for c in (rim_low, rim_high, wind_low, wind_high):
        c.wait()
    row = forward(t0, t1)
    row(wide - 2, True)
    row(wide - 1, False)
    row(0, True)
    low1 = send(t1.at[pl.ds(wide, 2)], t1.at[pl.ds(0, 2)], 5, flat(1))
    high1 = send(t1.at[pl.ds(2, 1)], t1.at[pl.ds(wide + 2, 1)], 6, flat(-1))
    run(1, wide - 2, row)
    observe(0)
    row = forward(t1, None)
    row(2, True)
    run(3, wide - 1, row)
    low1.wait()
    high1.wait()
    row(0, True)
    row(1, False)
    row(wide - 1, True)
    observe(1)

    spread(1)

    def back_yv(x, a, dst):
        a = each(mixed, each(lambda p, q: p + q, a, get_force(x)), get(mixx, x))
        q = each(lambda c, p, r: c * (p - r), get(cyx, x), ahead(a), a)
        put(dst, x + 2, each(gather_back, a, behind(q), q, ahead(q)))

    def first_back(x, fresh):
        back_yv(x, get(adjx, x), b1)

    def back_x(src, x, fresh):
        here = get(src, x + 2)
        after = get(src, x + 3)
        diff = lambda c, p, r: c * (p - r)
        if fresh:
            q_before = each(diff, get(cx, x), here, get(src, x + 1))
            q_here = each(diff, get(cx, x + 1), after, here)
            put(lines, x, q_before)
            put(lines, x + 1, q_here)
        else:
            q_before = get(lines, x)
            q_here = get(lines, x + 1)
        q_after = each(diff, get(cx, x + 2), get(src, x + 4), after)
        put(lines, x + 2, q_after)
        return each(gather_back, here, q_before, q_here, q_after)

    def rims_back(buf, k):
        return (
            send(buf.at[pl.ds(wide + 1, 1)], buf.at[pl.ds(1, 1)], k, flat(1)),
            send(buf.at[pl.ds(2, 2)], buf.at[pl.ds(wide + 2, 2)], k + 1, flat(-1)),
        )

    for x in (0, 1, wide - 1):
        first_back(x, True)
    rims = rims_back(b1, 7)
    run(2, wide - 1, first_back)
    spread(0)
    for c in rims:
        c.wait()

    def second_back(x, fresh):
        back_yv(x, back_x(b1, x, fresh), b0)

    second_back(wide - 1, True)
    second_back(0, True)
    second_back(1, False)
    rims = rims_back(b0, 9)
    run(2, wide - 1, second_back)

    def last(x, fresh):
        v = back_x(b0, x, fresh)
        for j in range(bands):
            made[j, pl.ds(x, levels, stride=wide), :] = v[j]

    last(1, True)
    run(2, wide - 2, last)
    for c in rims:
        c.wait()
    last(0, True)
    last(wide - 2, True)
    last(wide - 1, False)
    stores = [
        pltpu.make_async_copy(
            made.at[j], out.at[:, pl.ds(j * LANES, LANES)], load_sem.at[5, j]
        )
        for j in range(bands)
    ]
    for c in stores:
        c.start()
    await_all(stores)


def on_device(
    groups,
    tiles,
    checkpoint,
    adjoint_in,
    courant_x,
    courant_y,
    mixing,
    snd_column,
    snd_count,
    snd_step,
    snd_value,
    snd_weight,
    snd_kernel,
):
    levels, wide, long = checkpoint.shape
    cap = snd_column.shape[2]
    per = next(k for k in (PER, 2, 1) if tiles % k == 0)
    f32 = jnp.float32
    plane = (levels * wide, long)
    bands = long // LANES
    banded = (bands, levels * wide, LANES)
    rimmed = (wide + 4, levels, long)
    anywhere = pl.BlockSpec(memory_space=ANY)
    result = pl.pallas_call(
        functools.partial(kernel, groups, tiles, levels, wide, long, cap, per),
        out_shape=jax.ShapeDtypeStruct(plane, f32),
        in_specs=[anywhere] * 11,
        out_specs=anywhere,
        scratch_shapes=[
            pltpu.VMEM(banded, f32),
            pltpu.VMEM(banded, f32),
            pltpu.VMEM(banded, f32),
            pltpu.VMEM(banded, f32),
            pltpu.VMEM(banded, f32),
            pltpu.VMEM(banded, f32),
            pltpu.VMEM((3, levels, long), f32),
            pltpu.VMEM((wide + 2, levels, long), f32),
            pltpu.VMEM(rimmed, f32),
            pltpu.VMEM(rimmed, f32),
            pltpu.VMEM(rimmed, f32),
            pltpu.VMEM(rimmed, f32),
            pltpu.VMEM((wide, levels, long), f32),
            pltpu.VMEM((2 * levels * wide, long), jnp.bfloat16),
            pltpu.VMEM((tiles // per, long, per * cap), jnp.bfloat16),
            pltpu.VMEM((wide, levels, long), f32),
            pltpu.VMEM((wide, levels, long), f32),
            pltpu.VMEM((wide, levels, long), f32),
            pltpu.VMEM((1, levels, long), f32),
            pltpu.VMEM((wide + 2, levels, long), f32),
            pltpu.VMEM((tiles, levels, cap), f32),
            pltpu.VMEM((tiles, 8, cap), f32),
            pltpu.VMEM((tiles, 8, cap), f32),
            pltpu.VMEM((tiles // per, 8, per * cap), f32),
            pltpu.VMEM(banded, f32),
            pltpu.VMEM((tiles, cap), jnp.int32),
            pltpu.SMEM((1, tiles), jnp.int32),
            pltpu.VMEM((tiles, cap), jnp.int32),
            pltpu.VMEM((tiles, cap), f32),
            pltpu.VMEM((tiles, cap), f32),
            pltpu.SemaphoreType.DMA((5,)),
            pltpu.SemaphoreType.DMA((6, bands)),
            pltpu.SemaphoreType.DMA((11 + bands,)),
            pltpu.SemaphoreType.DMA((11 + bands,)),
            pltpu.SemaphoreType.DMA((2, tiles)),
            pltpu.SemaphoreType.DMA((2, tiles)),
        ],
        compiler_params=pltpu.CompilerParams(
            collective_id=0, has_side_effects=True, vmem_limit_bytes=48 * 1024 * 1024
        ),
        name="window",
    )(
        *(
            pltpu.with_memory_space_constraint(v, pltpu.HBM)
            for v in (
                checkpoint.reshape(plane),
                adjoint_in.reshape(plane),
                courant_x.reshape(plane),
                courant_y.reshape(plane),
                mixing.reshape(-1, long),
                snd_column.reshape(tiles, cap),
                snd_count,
                snd_step.reshape(tiles, cap),
                snd_value.reshape(tiles, cap),
                snd_weight.reshape(tiles, cap),
                snd_kernel.reshape(tiles, levels, cap),
            )
        )
    )
    return result.reshape(checkpoint.shape)


def solution(mesh):
    return jax.shard_map(
        functools.partial(on_device, mesh.shape["group"], mesh.shape["tile"]),
        mesh=mesh,
        in_specs=(
            P(None, ("group", "tile"), None),
            P(None, ("group", "tile"), None),
            P(None, ("group", "tile"), None),
            P(None, ("group", "tile"), None),
            P(None, ("group", "tile"), None),
            P(("group", "tile"), None, None),
            P(("group", "tile"), None),
            P(("group", "tile"), None, None),
            P(("group", "tile"), None, None),
            P(("group", "tile"), None, None),
            P(("group", "tile"), None, None, None),
        ),
        out_specs=P(None, ("group", "tile"), None),
        check_vma=False,
    )
```

```python
import functools

import jax
import jax.numpy as jnp
from jax import lax
from jax.experimental import pallas as pl
from jax.experimental.pallas import tpu as pltpu
from jax.sharding import PartitionSpec as P

STEPS = 2
MESH = pl.DeviceIdType.MESH
ANY = pltpu.HBM
LANES = 128
PER = 4
SIXTH = 1.0 / 6.0


def split_parts(v):
    high = v.astype(jnp.bfloat16)
    low = (v - high.astype(jnp.float32)).astype(jnp.bfloat16)
    return high, low


def kernel(
    groups,
    tiles,
    levels,
    wide,
    long,
    cap,
    per,
    chk_in,
    adj_in,
    cx_in,
    cy_in,
    mix_in,
    col_in,
    count_in,
    step_in,
    value_in,
    weight_in,
    kern_in,
    out,
    own,
    landed,
    adj,
    cxl,
    cy,
    mix,
    stage,
    cx,
    t0,
    t1,
    b1,
    b0,
    force,
    parts,
    onehot,
    cyx,
    mixx,
    adjx,
    line,
    lines,
    swept,
    kern,
    small,
    pack,
    misfit,
    made,
    col,
    count,
    step,
    value,
    weight,
    light_sem,
    load_sem,
    send_sem,
    recv_sem,
    snd_send,
    snd_recv,
):
    total = groups * tiles
    g = lax.axis_index("group")
    t = lax.axis_index("tile")
    me = g * tiles + t
    chunks = tiles // per
    width = per * cap

    def flat(offset):
        f = lax.rem(me + offset + total, total)
        return (lax.div(f, tiles), lax.rem(f, tiles))

    def partner(k):
        return (g, lax.rem(t + k, tiles))

    light = [
        pltpu.make_async_copy(src, dst, light_sem.at[k])
        for k, (src, dst) in enumerate(
            (
                (col_in, col),
                (count_in, count),
                (step_in, step),
                (value_in, value),
                (weight_in, weight),
            )
        )
    ]
    for c in light:
        c.start()
    bands = long // LANES
    loads = []
    for k, (src, dst) in enumerate(
        ((chk_in, own), (cx_in, cxl), (cy_in, cy), (mix_in, mix), (adj_in, adj))
    ):
        rows = src.shape[0]
        loads.append(
            [
                pltpu.make_async_copy(
                    src.at[:, pl.ds(j * LANES, LANES)],
                    dst.at[j, pl.ds(0, rows)],
                    load_sem.at[k, j],
                )
                for j in range(bands)
            ]
        )
        for c in loads[-1]:
            c.start()

    def await_all(copies):
        for c in copies:
            c.wait()

    barrier = pltpu.get_barrier_semaphore()
    roles = [flat(o) for o in (1, -1, tiles, tiles + 1, tiles - 1, -tiles, -tiles - 1, 1 - tiles)]
    roles += [partner(k) for k in range(1, tiles)]
    for role in roles:
        pl.semaphore_signal(barrier, inc=1, device_id=role, device_id_type=MESH)

    mix[:, pl.ds((levels - 1) * wide, wide), :] = jnp.zeros((bands, wide, LANES), jnp.float32)

    def column(ref, x):
        return jnp.concatenate(
            [ref[j, pl.ds(x, levels, stride=wide), :] for j in range(bands)], axis=1
        )

    pl.semaphore_wait(barrier, len(roles))

    def send(src, dst, k, to):
        c = pltpu.make_async_remote_copy(
            src_ref=src,
            dst_ref=dst,
            send_sem=send_sem.at[k],
            recv_sem=recv_sem.at[k],
            device_id=to,
            device_id_type=MESH,
        )
        c.start()
        return c

    main = [
        send(chk_in.at[:, pl.ds(j * LANES, LANES)], landed.at[j], 11 + j, flat(tiles))
        for j in range(bands)
    ]

    await_all(light)
    place = lax.broadcasted_iota(jnp.int32, (1, cap), 1)
    for k in range(tiles):
        pack[k, 0:1, :] = value[k : k + 1, :]
        pack[k, 1:2, :] = jnp.where(place < count[0, k], weight[k : k + 1, :], 0.0)
        pack[k, 2:3, :] = col[k : k + 1, :].astype(jnp.float32)
        pack[k, 3:4, :] = step[k : k + 1, :].astype(jnp.float32)

    snd = []
    for k in range(1, tiles):
        to = partner(k)
        for j, (src, dst) in enumerate(
            ((kern_in.at[to[1]], kern.at[k]), (pack.at[to[1]], small.at[k]))
        ):
            c = pltpu.make_async_remote_copy(
                src_ref=src,
                dst_ref=dst,
                send_sem=snd_send.at[j, k],
                recv_sem=snd_recv.at[j, k],
                device_id=to,
                device_id_type=MESH,
            )
            c.start()
            snd.append(c)
    for j, (src, dst) in enumerate(((kern_in.at[t], kern.at[0]), (pack.at[t], small.at[0]))):
        c = pltpu.make_async_copy(src, dst, snd_recv.at[j, 0])
        c.start()
        snd.append(c)

    await_all(loads[0])
    stage[0] = column(own, wide - 2)
    stage[1] = column(own, wide - 1)
    stage[2] = column(own, 0)
    rim_low = send(stage.at[pl.ds(0, 2)], t0.at[pl.ds(0, 2)], 1, flat(tiles + 1))
    rim_high = send(stage.at[pl.ds(2, 1)], t0.at[pl.ds(wide + 2, 1)], 2, flat(tiles - 1))
    await_all(loads[1])

    def turn(x, _):
        cx[x + 1] = column(cxl, x) * SIXTH
        return 0

    def turn_rest(x, _):
        cyx[x] = column(cy, x) * SIXTH
        mixx[x] = column(mix, x)
        adjx[x] = column(adj, x)
        return 0

    lax.fori_loop(0, wide, turn, 0)
    wind_low = send(cx.at[pl.ds(wide, 1)], cx.at[pl.ds(0, 1)], 3, flat(1))
    wind_high = send(cx.at[pl.ds(1, 1)], cx.at[pl.ds(wide + 1, 1)], 4, flat(-1))

    def row_of(c, r):
        return jnp.concatenate([small[c * per + k, r : r + 1, :] for k in range(per)], axis=1)

    def kern_of(c):
        return jnp.concatenate([kern[c * per + k] for k in range(per)], axis=1)

    def cell_of(c):
        cell = row_of(c, 2).astype(jnp.int32)
        cx_of = jnp.zeros_like(cell)
        for x in range(1, wide):
            cx_of = cx_of + jnp.where(cell >= x * long, 1, 0)
        return cx_of, cell - cx_of * long

    def mark(c, _):
        _, cy_of = cell_of(c)
        rows = 128
        for first in range(0, long, rows):
            at = lax.broadcasted_iota(jnp.int32, (rows, width), 0) + first
            onehot[c, first : first + rows, :] = jnp.where(at == cy_of, 1.0, 0.0).astype(
                jnp.bfloat16
            )
        return 0

    lane = lax.broadcasted_iota(jnp.int32, (levels, LANES), 1)
    at_first = lane == 0
    at_last = lane == LANES - 1

    def get(ref, x):
        return [ref[x, :, j * LANES : (j + 1) * LANES] for j in range(bands)]

    def put(ref, x, v):
        for j in range(bands):
            ref[x, :, j * LANES : (j + 1) * LANES] = v[j]

    def each(f, *lists):
        return [f(*items) for items in zip(*lists)]

    def ahead(v):
        r = [pltpu.roll(b, LANES - 1, 1) for b in v]
        return [jnp.where(at_last, r[(j + 1) % bands], r[j]) for j in range(bands)]

    def behind(v):
        r = [pltpu.roll(b, 1, 1) for b in v]
        return [jnp.where(at_first, r[j - 1], r[j]) for j in range(bands)]

    def mixed(v, m):
        f = m * (pltpu.roll(v, levels - 1, 0) - v)
        return v + f - pltpu.roll(f, 1, 0)

    def flux(c, after, here, before):
        return c * (2.0 * after + 5.0 * here - before)

    def gather_back(a, before, here, after):
        return a + 2.0 * before + 5.0 * here - after

    def along_y(x, v, dst):
        f = each(flux, get(cyx, x), ahead(v), v, behind(v))
        v = each(lambda p, q, r: p + q - r, v, behind(f), f)
        at = pl.multiple_of(x * 2 * levels, 2 * levels)
        for j, (b, m) in enumerate(zip(v, get(mixx, x))):
            b = mixed(b, m)
            across = slice(j * LANES, (j + 1) * LANES)
            if dst is not None:
                dst[x + 2, :, across] = b
            high, low = split_parts(b)
            parts[pl.ds(at, levels), across] = high
            parts[pl.ds(at + levels, levels), across] = low

    def forward(src, dst):
        def row(x, fresh):
            if fresh:
                lead = each(flux, get(cx, x), get(src, x + 2), get(src, x + 1), get(src, x))
            else:
                lead = get(line, 0)
            here = get(src, x + 2)
            trail = each(flux, get(cx, x + 1), get(src, x + 3), here, get(src, x + 1))
            put(line, 0, trail)
            along_y(x, each(lambda p, q, r: p + q - r, here, lead, trail), dst)

        return row

    def run(first, last, row):
        def body(x, _):
            row(x, False)
            return 0

        lax.fori_loop(first, last, body, 0)

    def observe(moment):
        def one(c, _):
            picked = jnp.dot(parts[...], onehot[c], preferred_element_type=jnp.float32)
            cx_of, _ = cell_of(c)
            seen = jnp.zeros((2 * levels, width), jnp.float32)
            for x in range(wide):
                seen = seen + jnp.where(
                    cx_of == x, picked[x * 2 * levels : (x + 1) * 2 * levels], 0.0
                )
            seen = seen[:levels] + seen[levels:]
            seen = jnp.sum(seen * kern_of(c), axis=0, keepdims=True)
            gap = row_of(c, 1) * (seen - row_of(c, 0))
            misfit[c, moment : moment + 1, :] = jnp.where(
                row_of(c, 3).astype(jnp.int32) == moment, gap, 0.0
            )
            return 0

        lax.fori_loop(0, chunks, one, 0)

    def spread(moment):
        def one(c, first):
            high, low = split_parts(kern_of(c) * misfit[c, moment : moment + 1, :])
            high, low = high.astype(jnp.float32), low.astype(jnp.float32)
            cx_of, _ = cell_of(c)
            rows = []
            for x in range(wide):
                for part in (high, low):
                    rows.append(jnp.where(cx_of == x, part, 0.0).astype(jnp.bfloat16))
            sums = lax.dot_general(
                jnp.concatenate(rows, axis=0),
                onehot[c],
                (((1,), (1,)), ((), ())),
                preferred_element_type=jnp.float32,
            )
            for x in range(wide):
                at = 2 * x * levels
                v = sums[at : at + levels] + sums[at + levels : at + 2 * levels]
                force[x] = v if first else force[x] + v

        one(0, True)

        def more(c, _):
            one(c, False)
            return 0

        if chunks > 1:
            lax.fori_loop(1, chunks, more, 0)

    def get_force(x):
        return get(force, x)

    for k in (2, 3, 4):
        await_all(loads[k])
    lax.fori_loop(0, wide, turn_rest, 0)

    await_all(snd)
    lax.fori_loop(0, chunks, mark, 0)
    for c in (wind_low, wind_high):
        c.wait()

    def sweep_x(x, across):
        lead = flux(cx[x, :, across], t0[x + 2, :, across], t0[x + 1, :, across], t0[x, :, across])
        here = t0[x + 2, :, across]
        trail = flux(cx[x + 1, :, across], t0[x + 3, :, across], here, t0[x + 1, :, across])
        swept[x, :, across] = here + lead - trail

    for j in range(bands):
        across = slice(j * LANES, (j + 1) * LANES)
        main[j].wait()
        for x in range(wide):
            t0[x + 2, :, across] = landed[j, pl.ds(x, levels, stride=wide), :]
        for x in range(2, wide - 1):
            sweep_x(x, across)
    rim_low.wait()
    rim_high.wait()
    for x in (0, 1, wide - 1):
        for j in range(bands):
            sweep_x(x, slice(j * LANES, (j + 1) * LANES))

    def first_forward(x, fresh):
        along_y(x, get(swept, x), t1)

    first_forward(wide - 2, False)
    first_forward(wide - 1, False)
    first_forward(0, False)
    low1 = send(t1.at[pl.ds(wide, 2)], t1.at[pl.ds(0, 2)], 5, flat(1))
    high1 = send(t1.at[pl.ds(2, 1)], t1.at[pl.ds(wide + 2, 1)], 6, flat(-1))
    run(1, wide - 2, first_forward)
    observe(0)
    row = forward(t1, None)
    row(2, True)
    run(3, wide - 1, row)
    low1.wait()
    high1.wait()
    row(0, True)
    row(1, False)
    row(wide - 1, True)
    observe(1)

    spread(1)

    def back_yv(x, a, dst):
        a = each(mixed, each(lambda p, q: p + q, a, get_force(x)), get(mixx, x))
        q = each(lambda c, p, r: c * (p - r), get(cyx, x), ahead(a), a)
        put(dst, x + 2, each(gather_back, a, behind(q), q, ahead(q)))

    def first_back(x, fresh):
        back_yv(x, get(adjx, x), b1)

    def back_x(src, x, fresh):
        here = get(src, x + 2)
        after = get(src, x + 3)
        diff = lambda c, p, r: c * (p - r)
        if fresh:
            q_before = each(diff, get(cx, x), here, get(src, x + 1))
            q_here = each(diff, get(cx, x + 1), after, here)
            put(lines, x, q_before)
            put(lines, x + 1, q_here)
        else:
            q_before = get(lines, x)
            q_here = get(lines, x + 1)
        q_after = each(diff, get(cx, x + 2), get(src, x + 4), after)
        put(lines, x + 2, q_after)
        return each(gather_back, here, q_before, q_here, q_after)

    def rims_back(buf, k):
        return (
            send(buf.at[pl.ds(wide + 1, 1)], buf.at[pl.ds(1, 1)], k, flat(1)),
            send(buf.at[pl.ds(2, 2)], buf.at[pl.ds(wide + 2, 2)], k + 1, flat(-1)),
        )

    for x in (0, 1, wide - 1):
        first_back(x, True)
    rims = rims_back(b1, 7)
    run(2, wide - 1, first_back)
    spread(0)
    for c in rims:
        c.wait()

    def second_back(x, fresh):
        back_yv(x, back_x(b1, x, fresh), b0)

    second_back(wide - 1, True)
    second_back(0, True)
    second_back(1, False)
    rims = rims_back(b0, 9)
    run(2, wide - 1, second_back)

    def last(x, fresh):
        v = back_x(b0, x, fresh)
        for j in range(bands):
            made[j, pl.ds(x, levels, stride=wide), :] = v[j]

    last(1, True)
    run(2, wide - 2, last)
    for c in rims:
        c.wait()
    last(0, True)
    last(wide - 2, True)
    last(wide - 1, False)
    stores = [
        pltpu.make_async_copy(
            made.at[j], out.at[:, pl.ds(j * LANES, LANES)], load_sem.at[5, j]
        )
        for j in range(bands)
    ]
    for c in stores:
        c.start()
    await_all(stores)


def on_device(
    groups,
    tiles,
    checkpoint,
    adjoint_in,
    courant_x,
    courant_y,
    mixing,
    snd_column,
    snd_count,
    snd_step,
    snd_value,
    snd_weight,
    snd_kernel,
):
    levels, wide, long = checkpoint.shape
    cap = snd_column.shape[2]
    per = next(k for k in (PER, 2, 1) if tiles % k == 0)
    f32 = jnp.float32
    plane = (levels * wide, long)
    bands = long // LANES
    banded = (bands, levels * wide, LANES)
    rimmed = (wide + 4, levels, long)
    anywhere = pl.BlockSpec(memory_space=ANY)
    result = pl.pallas_call(
        functools.partial(kernel, groups, tiles, levels, wide, long, cap, per),
        out_shape=jax.ShapeDtypeStruct(plane, f32),
        in_specs=[anywhere] * 11,
        out_specs=anywhere,
        scratch_shapes=[
            pltpu.VMEM(banded, f32),
            pltpu.VMEM(banded, f32),
            pltpu.VMEM(banded, f32),
            pltpu.VMEM(banded, f32),
            pltpu.VMEM(banded, f32),
            pltpu.VMEM(banded, f32),
            pltpu.VMEM((3, levels, long), f32),
            pltpu.VMEM((wide + 2, levels, long), f32),
            pltpu.VMEM(rimmed, f32),
            pltpu.VMEM(rimmed, f32),
            pltpu.VMEM(rimmed, f32),
            pltpu.VMEM(rimmed, f32),
            pltpu.VMEM((wide, levels, long), f32),
            pltpu.VMEM((2 * levels * wide, long), jnp.bfloat16),
            pltpu.VMEM((tiles // per, long, per * cap), jnp.bfloat16),
            pltpu.VMEM((wide, levels, long), f32),
            pltpu.VMEM((wide, levels, long), f32),
            pltpu.VMEM((wide, levels, long), f32),
            pltpu.VMEM((1, levels, long), f32),
            pltpu.VMEM((wide + 2, levels, long), f32),
            pltpu.VMEM((wide, levels, long), f32),
            pltpu.VMEM((tiles, levels, cap), f32),
            pltpu.VMEM((tiles, 8, cap), f32),
            pltpu.VMEM((tiles, 8, cap), f32),
            pltpu.VMEM((tiles // per, 8, per * cap), f32),
            pltpu.VMEM(banded, f32),
            pltpu.VMEM((tiles, cap), jnp.int32),
            pltpu.SMEM((1, tiles), jnp.int32),
            pltpu.VMEM((tiles, cap), jnp.int32),
            pltpu.VMEM((tiles, cap), f32),
            pltpu.VMEM((tiles, cap), f32),
            pltpu.SemaphoreType.DMA((5,)),
            pltpu.SemaphoreType.DMA((6, bands)),
            pltpu.SemaphoreType.DMA((11 + bands,)),
            pltpu.SemaphoreType.DMA((11 + bands,)),
            pltpu.SemaphoreType.DMA((2, tiles)),
            pltpu.SemaphoreType.DMA((2, tiles)),
        ],
        compiler_params=pltpu.CompilerParams(
            collective_id=0, has_side_effects=True, vmem_limit_bytes=48 * 1024 * 1024
        ),
        name="window",
    )(
        *(
            pltpu.with_memory_space_constraint(v, pltpu.HBM)
            for v in (
                checkpoint.reshape(plane),
                adjoint_in.reshape(plane),
                courant_x.reshape(plane),
                courant_y.reshape(plane),
                mixing.reshape(-1, long),
                snd_column.reshape(tiles, cap),
                snd_count,
                snd_step.reshape(tiles, cap),
                snd_value.reshape(tiles, cap),
                snd_weight.reshape(tiles, cap),
                snd_kernel.reshape(tiles, levels, cap),
            )
        )
    )
    return result.reshape(checkpoint.shape)


def solution(mesh):
    return jax.shard_map(
        functools.partial(on_device, mesh.shape["group"], mesh.shape["tile"]),
        mesh=mesh,
        in_specs=(
            P(None, ("group", "tile"), None),
            P(None, ("group", "tile"), None),
            P(None, ("group", "tile"), None),
            P(None, ("group", "tile"), None),
            P(None, ("group", "tile"), None),
            P(("group", "tile"), None, None),
            P(("group", "tile"), None),
            P(("group", "tile"), None, None),
            P(("group", "tile"), None, None),
            P(("group", "tile"), None, None),
            P(("group", "tile"), None, None, None),
        ),
        out_specs=P(None, ("group", "tile"), None),
        check_vma=False,
    )
```
